32 devices in a mesh: rows: 8 (over y, x, core), draws: 4 (over z).
Axes of the slice: x: 2, y: 2, z: 4, core: 2. Of those that a mesh axis runs over, the one named last changes fastest.
Arguments:
- pool_inputs: bfloat16 [2048, 4096], P('rows', 'draws'), may hold values from -8 to 8
- target_inputs: bfloat16 [2048, 4096], P('rows', 'draws'), may hold values from -8 to 8
- class_weights: bfloat16 [4096, 4096], P(None, 'draws'), may hold values from -1 to 1
- class_bias: float32 [4096], P('draws'), may hold values from -6 to 6
Outputs:
- gain: float32 [2048], P('rows')
The draws below stay inside these ranges and needn't reach their ends.
All inputs are finite; a program needn't handle non-finite values.
Results may differ from the reference program's by a relative error of at most 0.003.
Values may be sent and summed in bfloat16 or wider, within the bound.
A program may use at most 64 MiB of HBM per device.

```python
import math
import jax
import jax.numpy as jnp
from jax import lax

F = 4096
C = 16
K = 256
POOL = 2048
TARGETS = 2048


def row_inputs(key, count, salt):
    sub = jax.random.fold_in(key, salt)
    first_key, second_key = jax.random.split(sub, 2)
    base = jax.random.normal(first_key, (count, F), jnp.float32)
    scales = jnp.exp(jax.random.uniform(second_key, (count,), jnp.float32, -0.6931472, 0.6931472))
    values = base * scales[:, None]
    return jnp.clip(values, -8.0, 8.0)


def draw_pool_inputs(key, part):
    return row_inputs(key, POOL, 1).astype(jnp.bfloat16)


def draw_target_inputs(key, part):
    return row_inputs(key, TARGETS, 2).astype(jnp.bfloat16)


def draw_class_weights(key, part):
    sub = jax.random.fold_in(key, 3)
    keys = jax.random.split(sub, 1)
    base = jax.random.normal(keys[0], (F, K * C), jnp.float32) * (3.0 / F ** 0.5)
    return jnp.clip(base, -1.0, 1.0).astype(jnp.bfloat16)


def level_of(rng, dims, pieces, low, largest):
    level = 1.0
    for axis_at, shards_of in pieces:
        heights = jax.random.uniform(jax.random.fold_in(jax.random.fold_in(rng, 6), axis_at), (shards_of,), jnp.float32, low / len(pieces), largest / len(pieces))
        level = level * jnp.repeat(jnp.exp(heights), dims[axis_at] // shards_of).reshape((-1,) + (1,) * (len(dims) - 1 - axis_at))
    return level


def scatter_about(key, shape, spread, reach, cuts=(), kind=jnp.bfloat16):
    level = level_of(key, shape, cuts, -0.22, 0.18) if cuts else 1.0
    values = jax.random.normal(key, shape, jnp.float32) * spread * level
    return jnp.minimum(jnp.maximum(values, -reach), reach).astype(kind)


def setup_inputs(seed: int = 0) -> dict:
    key_of = jax.random.split(jax.random.key(seed), 5)
    pool_inputs = draw_pool_inputs(jax.random.fold_in(key_of[4], 71), 0)
    target_inputs = draw_target_inputs(jax.random.fold_in(key_of[4], 71), 0)
    class_weights = draw_class_weights(jax.random.fold_in(key_of[4], 71), 0)
    class_bias = scatter_about(key_of[3], (K * C,), 1.0, 6.0, ((0, 4),), jnp.float32)
    return dict(pool_inputs=pool_inputs, target_inputs=target_inputs, class_weights=class_weights, class_bias=class_bias)


def probabilities(inputs, class_weights, class_bias):
    logits = jnp.dot(inputs, class_weights, preferred_element_type=jnp.float32) + class_bias
    count = inputs.shape[0]
    probs = jax.nn.softmax(logits.reshape(count, K, C), axis=-1)
    return jnp.transpose(probs, (1, 0, 2)).reshape(K, count * C).astype(jnp.bfloat16)


def entropy_of(probs, count):
    ones = jnp.ones((K,), jnp.bfloat16)
    mean = (jnp.dot(ones, probs, preferred_element_type=jnp.float32) / K).reshape(count, C)
    return -jnp.sum(jax.scipy.special.xlogy(mean, mean), axis=-1)


def reference(pool_inputs, target_inputs, class_weights, class_bias):
    pool_probs = probabilities(pool_inputs, class_weights, class_bias)
    target_probs = probabilities(target_inputs, class_weights, class_bias)
    pool_entropy = entropy_of(pool_probs, POOL)
    target_entropy = entropy_of(target_probs, TARGETS)
    pool_block = math.gcd(POOL, 256)
    target_block = math.gcd(TARGETS, 512)
    pool_parts = jnp.transpose(pool_probs.reshape(K, POOL // pool_block, pool_block * C), (1, 0, 2))
    target_parts = jnp.transpose(target_probs.reshape(K, TARGETS // target_block, target_block * C), (1, 0, 2))

    def per_pool(pool_piece):
        def per_target(total, target_piece):
            joint = jnp.dot(pool_piece.T, target_piece, preferred_element_type=jnp.float32) / K
            joint = joint.reshape(pool_block, C, target_block, C)
            return total + jnp.sum(jax.scipy.special.xlogy(joint, joint), axis=(1, 2, 3)), None

        total, _ = lax.scan(per_target, jnp.zeros((pool_block,), jnp.float32), target_parts)
        return total

    sums = lax.map(per_pool, pool_parts).reshape(POOL)
    return sums / TARGETS + pool_entropy + jnp.sum(target_entropy) / TARGETS
```

```python
import functools

import jax
import jax.numpy as jnp
from jax import lax
from jax.experimental import pallas as pl
from jax.experimental.pallas import tpu as pltpu
from jax.sharding import PartitionSpec as P

C = 16
LANES = 128
MESH = pl.DeviceIdType.MESH
TINY = 1.1754944e-38


def xlogx(value):
    return value * jnp.log(jnp.maximum(value, TINY))


def kernel(
    R, D, pool_ref, target_ref, weights_ref, bias_ref, out_ref,
    w, gx, logits, turned, target_local, pool_full, pool_turned, target_full,
    joint_sum, totals, stage, final,
    in_sem, f_send, f_recv, a_send, a_recv, r_send, r_recv, c_send, c_recv,
    p_send, p_recv, l_sem, t_send, t_recv,
):
    r = lax.axis_index("rows")
    z = lax.axis_index("draws")
    rows, depth = gx.shape[2], gx.shape[3]
    columns = w.shape[1]
    heads = columns // C
    K = heads * D
    part = rows // D
    fold = LANES // part
    groups = C // fold
    halves = rows // LANES
    partner = r + 1 - 2 * lax.rem(r, 2)
    pairs = R // 2
    has_right = z < D - 1
    has_left = z > 0

    inputs = (target_ref, pool_ref)

    def load(a):
        return pltpu.make_async_copy(inputs[a], gx.at[a, z], in_sem.at[a])

    load_w = pltpu.make_async_copy(weights_ref, w, in_sem.at[2])
    load(0).start()
    load(1).start()
    load_w.start()

    barrier = pltpu.get_barrier_semaphore()
    for j in range(1, D):
        pl.semaphore_signal(barrier, inc=1, device_id=(r, lax.rem(z + j, D)), device_id_type=MESH)
    for j in range(1, pairs):
        pl.semaphore_signal(barrier, inc=1, device_id=(lax.rem(r + 2 * j, R), z), device_id_type=MESH)
    pl.semaphore_signal(barrier, inc=1, device_id=(partner, z), device_id_type=MESH)
    pl.semaphore_wait(barrier, D - 1 + pairs)

    def feature(a, way, hop, owner):
        return pltpu.make_async_remote_copy(
            src_ref=gx.at[a, owner],
            dst_ref=gx.at[a, owner],
            send_sem=f_send.at[a, way, hop],
            recv_sem=f_recv.at[a, way, hop],
            device_id=(r, z + 1 - 2 * way),
            device_id_type=MESH,
        )

    def share(j):
        there = lax.rem(z + j, D)
        return pltpu.make_async_remote_copy(
            src_ref=target_local.at[there],
            dst_ref=target_full.at[r, :, pl.ds(pl.multiple_of(z * heads, heads), heads), :],
            send_sem=a_send.at[j - 1],
            recv_sem=a_recv.at[j - 1],
            device_id=(r, there),
            device_id_type=MESH,
        )

    def share_in(j):
        there = lax.rem(z + D - j, D)
        at = pl.ds(pl.multiple_of(there * heads, heads), heads)
        return pltpu.make_async_remote_copy(
            src_ref=target_local.at[there],
            dst_ref=target_full.at[r, :, at, :],
            send_sem=a_send.at[j - 1],
            recv_sem=a_recv.at[j - 1],
            device_id=(r, there),
            device_id_type=MESH,
        )

    def share_own():
        return pltpu.make_async_copy(
            target_local.at[z],
            target_full.at[r, :, pl.ds(pl.multiple_of(z * heads, heads), heads), :],
            l_sem.at[0],
        )

    def across(j, piece, there):
        return pltpu.make_async_remote_copy(
            src_ref=target_full.at[piece],
            dst_ref=target_full.at[piece],
            send_sem=r_send.at[j - 1],
            recv_sem=r_recv.at[j - 1],
            device_id=(there, z),
            device_id_type=MESH,
        )

    def beside(j, piece):
        return pltpu.make_async_remote_copy(
            src_ref=target_full.at[piece],
            dst_ref=target_full.at[piece],
            send_sem=c_send.at[j],
            recv_sem=c_recv.at[j],
            device_id=(partner, z),
            device_id_type=MESH,
        )

    def pool_copy(way, hop, owner, chunk):
        at = pl.ds(pl.multiple_of(owner * heads, heads), heads)
        return pltpu.make_async_remote_copy(
            src_ref=pool_full.at[chunk, :, at, :],
            dst_ref=pool_full.at[chunk, :, at, :],
            send_sem=p_send.at[way, hop, chunk],
            recv_sem=p_recv.at[way, hop, chunk],
            device_id=(r, z + 1 - 2 * way),
            device_id_type=MESH,
        )

    wide = min(columns, 256)

    def multiply(a, owner, first):
        base = pl.multiple_of(owner * depth, depth)

        def tile(j, carry):
            at = pl.ds(pl.multiple_of(j * wide, wide), wide)
            product = jnp.dot(
                gx[a, owner], w[pl.ds(base, depth), at], preferred_element_type=jnp.float32
            )
            if first:
                logits[:, at] = product + bias_ref[:, at]
            else:
                logits[:, at] += product
            return carry

        lax.fori_loop(0, columns // wide, tile, 0)

    lane = lax.broadcasted_iota(jnp.int32, (16, LANES), 1)
    segment = lax.div(lane, part)

    def probabilities(store):
        def turn(j, carry):
            at = pl.ds(pl.multiple_of(j * LANES, LANES), LANES)
            for h in range(halves):
                turned[h, at, :] = logits[h * LANES : (h + 1) * LANES, at].T
            return carry

        lax.fori_loop(0, columns // LANES, turn, 0)

        def some(k, carry):
            for h in range(halves):
                values = [
                    turned[h, pl.ds(k * 16 * C + c, 16, stride=C), :] for c in range(C)
                ]
                top = functools.reduce(jnp.maximum, values)
                values = [jnp.exp(v - top) for v in values]
                scale = 1.0 / functools.reduce(jnp.add, values)
                values = [v * scale for v in values]
                for g in range(groups):
                    for q in range(fold):
                        mixed = values[g * fold]
                        if q:
                            mixed = pltpu.roll(mixed, (LANES - q * part) % LANES, 1)
                        for j in range(1, fold):
                            other = values[g * fold + j]
                            shift = ((j - q) * part) % LANES
                            if shift:
                                other = pltpu.roll(other, shift, 1)
                            mixed = jnp.where(segment == j, other, mixed)
                        store(h * fold + q, g, pl.multiple_of(k * 16, 16), mixed.astype(jnp.bfloat16))
            return carry

        lax.fori_loop(0, heads // 16, some, 0)

    def store_target(chunk, g, k, value):
        target_local[chunk, g, pl.ds(k, 16), :] = value

    def store_pool(chunk, g, k, value):
        pool_full[chunk, g, pl.ds(pl.multiple_of(z * heads + k, 16), 16), :] = value

    def start_own(a):
        @pl.when(has_right)
        def _():
            feature(a, 0, 0, z).start()

        @pl.when(has_left)
        def _():
            feature(a, 1, 0, z).start()

    def gather_step(a, s):
        @pl.when(z - s >= 0)
        def _():
            feature(a, 0, s - 1, z - s).wait_recv()

            @pl.when(has_right)
            def _():
                feature(a, 0, s, z - s).start()

        @pl.when(z + s <= D - 1)
        def _():
            feature(a, 1, s - 1, z + s).wait_recv()

            @pl.when(has_left)
            def _():
                feature(a, 1, s, z + s).start()

    def multiply_step(a, s):
        @pl.when(z - s >= 0)
        def _():
            multiply(a, z - s, False)

        @pl.when(z + s <= D - 1)
        def _():
            multiply(a, z + s, False)

    load(0).wait()
    start_own(0)
    load(1).wait()

    def start_pool(s):
        @pl.when((s == z) & has_right)
        def _():
            feature(1, 0, 0, z).start()

        @pl.when((s == D - 1 - z) & has_left)
        def _():
            feature(1, 1, 0, z).start()

    start_pool(0)
    load_w.wait()
    multiply(0, z, True)

    def target_step(s, carry):
        gather_step(0, s)
        start_pool(s)
        multiply_step(0, s)
        return carry

    lax.fori_loop(1, D, target_step, 0)
    probabilities(store_target)
    multiply(1, z, True)
    share_own().start()
    for j in range(1, D):
        share(j).start()

    def pool_step(s, carry):
        gather_step(1, s)
        multiply_step(1, s)

        @pl.when(s == max(1, D - 2))
        def _():
            share_own().wait()
            for j in range(1, D):
                share_in(j).wait_recv()
            for j in range(1, pairs):
                across(j, r, lax.rem(r + 2 * j, R)).start()
            beside(0, r).start()

        return carry

    lax.fori_loop(1, D, pool_step, 0)
    probabilities(store_pool)

    ones = jnp.ones((8, K), jnp.bfloat16)

    def fold_lanes(row):
        total = row
        for j in range(1, fold):
            total = total + pltpu.roll(row, j * part, 1)
        return total

    def entropy_rows(ref, first):
        def add(g, carry):
            mean = jnp.dot(ones, ref[first, g], preferred_element_type=jnp.float32) * (1.0 / K)
            return carry + xlogx(mean)

        return lax.fori_loop(0, groups, add, jnp.zeros((8, LANES), jnp.float32))

    def joint(chunk):
        def turn(g, carry):
            block = pool_full[chunk, g].T.astype(jnp.float32) * (1.0 / K)
            pool_turned[pl.ds(pl.multiple_of(g * LANES, LANES), LANES), :] = block.astype(
                jnp.bfloat16
            )
            return carry

        lax.fori_loop(0, groups, turn, 0)
        joint_sum[...] = jnp.zeros_like(joint_sum)
        double = 2 if groups % 2 == 0 else 1
        tall = min(256, groups * LANES)

        def column(i, carry):
            piece = lax.div(i, groups // double)
            g = lax.rem(i, groups // double) * double
            block = jnp.concatenate([target_full[piece, g + b] for b in range(double)], axis=1)
            total = None
            for top in range(0, groups * LANES, tall):
                value = xlogx(
                    jnp.dot(
                        pool_turned[top : top + tall, :], block, preferred_element_type=jnp.float32
                    )
                )
                for u in range(0, tall, LANES):
                    for v in range(0, double * LANES, LANES):
                        term = value[u : u + LANES, v : v + LANES]
                        total = term if total is None else total + term
            joint_sum[...] += total
            return carry

        lax.fori_loop(0, R * groups // double, column, 0)
        summed = jnp.sum(joint_sum[...].T, axis=0, keepdims=True)
        totals[0, chunk] = fold_lanes(jnp.broadcast_to(summed, (8, LANES)))
        totals[1, chunk] = fold_lanes(entropy_rows(pool_full, chunk))

    def finish_targets():
        for j in range(1, pairs):
            piece = lax.rem(r + R - 2 * j, R)
            across(j, piece, piece).wait_recv()
            beside(j, piece).start()
        for j in range(pairs):
            beside(j, lax.rem(partner + R - 2 * j, R)).wait_recv()

    def pool_round(t, carry):
        for s in range(D):
            chunk = t - s
            valid = (chunk >= 0) & (chunk < D)

            @pl.when(valid & (z - s >= 0))
            def _():
                if s:
                    pool_copy(0, s - 1, z - s, chunk).wait_recv()
                if s < D - 1:
                    @pl.when(has_right)
                    def _():
                        pool_copy(0, s, z - s, chunk).start()

            @pl.when(valid & (z + s <= D - 1))
            def _():
                if s:
                    pool_copy(1, s - 1, z + s, chunk).wait_recv()
                if s < D - 1:
                    @pl.when(has_left)
                    def _():
                        pool_copy(1, s, z + s, chunk).start()

        @pl.when(t == D - 1)
        def _():
            finish_targets()

        @pl.when(t >= D - 1)
        def _():
            joint(t - (D - 1))

        return carry

    lax.fori_loop(0, 2 * D - 1, pool_round, 0)

    def target_entropy(piece, carry):
        return carry + entropy_rows(target_full, piece)

    sums = lax.fori_loop(0, R, target_entropy, jnp.zeros((8, LANES), jnp.float32))
    targets_sum = jnp.sum(sums) * 0.125

    seg8 = lax.div(lax.broadcasted_iota(jnp.int32, (8, LANES), 1), part)

    def laid(which, h):
        row = totals[which, h * fold]
        for q in range(1, fold):
            row = jnp.where(seg8 == q, totals[which, h * fold + q], row)
        return row

    for h in range(halves):
        stage[h] = laid(0, h) - targets_sum
    keep = pltpu.make_async_copy(stage, final.at[z], l_sem.at[1])
    keep.start()
    keep.wait()

    def total_copy(j, owner, there):
        return pltpu.make_async_remote_copy(
            src_ref=final.at[owner],
            dst_ref=final.at[owner],
            send_sem=t_send.at[j - 1],
            recv_sem=t_recv.at[j - 1],
            device_id=(r, there),
            device_id_type=MESH,
        )

    for j in range(1, D):
        total_copy(j, z, lax.rem(z + j, D)).start()

    def ended(s, carry):
        for a in range(2):
            @pl.when((z - s >= 0) & has_right)
            def _():
                feature(a, 0, s, z - s).wait_send()

            @pl.when((z + s <= D - 1) & has_left)
            def _():
                feature(a, 1, s, z + s).wait_send()

        for chunk in range(D):
            @pl.when((z - s >= 0) & has_right)
            def _():
                pool_copy(0, s, z - s, chunk).wait_send()

            @pl.when((z + s <= D - 1) & has_left)
            def _():
                pool_copy(1, s, z + s, chunk).wait_send()

        return carry

    lax.fori_loop(0, D - 1, ended, 0)
    for j in range(1, D):
        share(j).wait_send()
    for j in range(1, pairs):
        across(j, r, lax.rem(r + 2 * j, R)).wait_send()
    for j in range(pairs):
        beside(j, lax.rem(r + R - 2 * j, R)).wait_send()
    for j in range(1, D):
        there = lax.rem(z + D - j, D)
        total_copy(j, there, there).wait_recv()
    for j in range(1, D):
        total_copy(j, z, lax.rem(z + j, D)).wait_send()
    scale = 1.0 / (R * part * D)
    for h in range(halves):
        total = final[0, h]
        for d in range(1, D):
            total = total + final[d, h]
        out_ref[h] = total * scale - laid(1, h)


def local(R, D, pool_inputs, target_inputs, class_weights, class_bias):
    rows, depth = pool_inputs.shape
    features, columns = class_weights.shape
    heads = columns // C
    K = heads * D
    part = rows // D
    fold = LANES // part
    groups = C // fold
    halves = rows // LANES
    bf16, f32 = jnp.bfloat16, jnp.float32
    DMA = pltpu.SemaphoreType.DMA
    anywhere = pl.BlockSpec(memory_space=pl.ANY)
    out = pl.pallas_call(
        functools.partial(kernel, R, D),
        out_shape=jax.ShapeDtypeStruct((halves, 8, LANES), f32),
        in_specs=[anywhere, anywhere, anywhere, pl.BlockSpec(memory_space=pltpu.VMEM)],
        out_specs=pl.BlockSpec(memory_space=pltpu.VMEM),
        scratch_shapes=[
            pltpu.VMEM((features, columns), bf16),
            pltpu.VMEM((2, D, rows, depth), bf16),
            pltpu.VMEM((rows, columns), f32),
            pltpu.VMEM((halves, columns, LANES), f32),
            pltpu.VMEM((D, groups, heads, LANES), bf16),
            pltpu.VMEM((D, groups, K, LANES), bf16),
            pltpu.VMEM((groups * LANES, K), bf16),
            pltpu.VMEM((R, groups, K, LANES), bf16),
            pltpu.VMEM((LANES, LANES), f32),
            pltpu.VMEM((2, D, 8, LANES), f32),
            pltpu.VMEM((halves, 8, LANES), f32),
            pltpu.VMEM((D, halves, 8, LANES), f32),
            DMA((3,)),
            DMA((2, 2, D - 1)),
            DMA((2, 2, D - 1)),
            DMA((D - 1,)),
            DMA((D - 1,)),
            DMA((R // 2 - 1,)),
            DMA((R // 2 - 1,)),
            DMA((R // 2,)),
            DMA((R // 2,)),
            DMA((2, D - 1, D)),
            DMA((2, D - 1, D)),
            DMA((2,)),
            DMA((D - 1,)),
            DMA((D - 1,)),
        ],
        compiler_params=pltpu.CompilerParams(collective_id=0, has_side_effects=True),
        name="gain",
    )(pool_inputs, target_inputs, class_weights, class_bias.reshape(1, columns))
    return out[:, 0, :].reshape(rows)


def solution(mesh):
    R, D = mesh.shape["rows"], mesh.shape["draws"]
    placed = (P("rows", "draws"), P("rows", "draws"), P(None, "draws"), P("draws"))
    return jax.shard_map(
        functools.partial(local, R, D),
        mesh=mesh,
        in_specs=placed,
        out_specs=P("rows"),
        check_vma=False,
    )
```

```python
import functools
import math

import jax
import jax.numpy as jnp
from jax import lax
from jax.experimental import pallas as pl
from jax.experimental.pallas import tpu as pltpu
from jax.sharding import PartitionSpec as P

C = 16
LANES = 128
MESH = pl.DeviceIdType.MESH
TINY = 1.1754944e-38


def xlogx(value):
    return value * jnp.log(jnp.maximum(value, TINY))


def kernel(
    R, D, pool_ref, target_ref, weights_ref, bias_ref, out_ref,
    w, gx, logits, turned, target_local, pool_full, pool_turned, target_full,
    joint_sum, totals, stage, final,
    in_sem, f_send, f_recv, a_send, a_recv, r_send, r_recv, c_send, c_recv,
    p_send, p_recv, l_sem, t_send, t_recv,
):
    r = lax.axis_index("rows")
    z = lax.axis_index("draws")
    rows, depth = gx.shape[2], gx.shape[3]
    columns = w.shape[1]
    heads = columns // C
    K = heads * D
    part = rows // D
    fold = LANES // part
    groups = C // fold
    halves = rows // LANES
    partner = r + 1 - 2 * lax.rem(r, 2)
    pairs = R // 2
    has_right = z < D - 1
    has_left = z > 0

    inputs = (target_ref, pool_ref)

    def load(a):
        return pltpu.make_async_copy(inputs[a], gx.at[a, z], in_sem.at[a])

    load_w = pltpu.make_async_copy(weights_ref, w, in_sem.at[2])
    load(0).start()
    load(1).start()
    load_w.start()

    barrier = pltpu.get_barrier_semaphore()
    for j in range(1, D):
        pl.semaphore_signal(barrier, inc=1, device_id=(r, lax.rem(z + j, D)), device_id_type=MESH)
    for j in range(1, pairs):
        pl.semaphore_signal(barrier, inc=1, device_id=(lax.rem(r + 2 * j, R), z), device_id_type=MESH)
    pl.semaphore_signal(barrier, inc=1, device_id=(partner, z), device_id_type=MESH)
    pl.semaphore_wait(barrier, D - 1 + pairs)

    def feature(a, way, hop, owner):
        return pltpu.make_async_remote_copy(
            src_ref=gx.at[a, owner],
            dst_ref=gx.at[a, owner],
            send_sem=f_send.at[a, way, hop],
            recv_sem=f_recv.at[a, way, hop],
            device_id=(r, z + 1 - 2 * way),
            device_id_type=MESH,
        )

    def share(j):
        there = lax.rem(z + j, D)
        return pltpu.make_async_remote_copy(
            src_ref=target_local.at[there],
            dst_ref=target_full.at[r, :, pl.ds(pl.multiple_of(z * heads, heads), heads), :],
            send_sem=a_send.at[j - 1],
            recv_sem=a_recv.at[j - 1],
            device_id=(r, there),
            device_id_type=MESH,
        )

    def share_in(j):
        there = lax.rem(z + D - j, D)
        at = pl.ds(pl.multiple_of(there * heads, heads), heads)
        return pltpu.make_async_remote_copy(
            src_ref=target_local.at[there],
            dst_ref=target_full.at[r, :, at, :],
            send_sem=a_send.at[j - 1],
            recv_sem=a_recv.at[j - 1],
            device_id=(r, there),
            device_id_type=MESH,
        )

    def share_own():
        return pltpu.make_async_copy(
            target_local.at[z],
            target_full.at[r, :, pl.ds(pl.multiple_of(z * heads, heads), heads), :],
            l_sem.at[0],
        )

    def across(j, piece, there):
        return pltpu.make_async_remote_copy(
            src_ref=target_full.at[piece],
            dst_ref=target_full.at[piece],
            send_sem=r_send.at[j - 1],
            recv_sem=r_recv.at[j - 1],
            device_id=(there, z),
            device_id_type=MESH,
        )

    def beside(j, piece):
        return pltpu.make_async_remote_copy(
            src_ref=target_full.at[piece],
            dst_ref=target_full.at[piece],
            send_sem=c_send.at[j],
            recv_sem=c_recv.at[j],
            device_id=(partner, z),
            device_id_type=MESH,
        )

    def pool_copy(way, hop, owner, chunk):
        at = pl.ds(pl.multiple_of(owner * heads, heads), heads)
        return pltpu.make_async_remote_copy(
            src_ref=pool_full.at[chunk, :, at, :],
            dst_ref=pool_full.at[chunk, :, at, :],
            send_sem=p_send.at[way, hop, chunk],
            recv_sem=p_recv.at[way, hop, chunk],
            device_id=(r, z + 1 - 2 * way),
            device_id_type=MESH,
        )

    wide = min(columns, 256)

    def multiply(a, owner, first):
        base = pl.multiple_of(owner * depth, depth)

        def tile(j, carry):
            at = pl.ds(pl.multiple_of(j * wide, wide), wide)
            product = jnp.dot(
                gx[a, owner], w[pl.ds(base, depth), at], preferred_element_type=jnp.float32
            )
            if first:
                logits[:, at] = product + bias_ref[:, at]
            else:
                logits[:, at] += product
            return carry

        lax.fori_loop(0, columns // wide, tile, 0)

    lane = lax.broadcasted_iota(jnp.int32, (16, LANES), 1)
    segment = lax.div(lane, part)

    def probabilities(store):
        def turn(j, carry):
            at = pl.ds(pl.multiple_of(j * LANES, LANES), LANES)
            for h in range(halves):
                turned[h, at, :] = logits[h * LANES : (h + 1) * LANES, at].T
            return carry

        lax.fori_loop(0, columns // LANES, turn, 0)

        def some(k, carry):
            for h in range(halves):
                values = [
                    turned[h, pl.ds(k * 16 * C + c, 16, stride=C), :] for c in range(C)
                ]
                top = functools.reduce(jnp.maximum, values)
                values = [jnp.exp(v - top) for v in values]
                scale = 1.0 / functools.reduce(jnp.add, values)
                values = [v * scale for v in values]
                for g in range(groups):
                    for q in range(fold):
                        mixed = values[g * fold]
                        if q:
                            mixed = pltpu.roll(mixed, (LANES - q * part) % LANES, 1)
                        for j in range(1, fold):
                            other = values[g * fold + j]
                            shift = ((j - q) * part) % LANES
                            if shift:
                                other = pltpu.roll(other, shift, 1)
                            mixed = jnp.where(segment == j, other, mixed)
                        store(h * fold + q, g, pl.multiple_of(k * 16, 16), mixed.astype(jnp.bfloat16))
            return carry

        lax.fori_loop(0, heads // 16, some, 0)

    def store_target(chunk, g, k, value):
        target_local[chunk, g, pl.ds(k, 16), :] = value

    def store_pool(chunk, g, k, value):
        pool_full[chunk, g, pl.ds(pl.multiple_of(z * heads + k, 16), 16), :] = value

    def start_own(a):
        @pl.when(has_right)
        def _():
            feature(a, 0, 0, z).start()

        @pl.when(has_left)
        def _():
            feature(a, 1, 0, z).start()

    def gather_step(a, s):
        @pl.when(z - s >= 0)
        def _():
            feature(a, 0, s - 1, z - s).wait_recv()

            @pl.when(has_right)
            def _():
                feature(a, 0, s, z - s).start()

        @pl.when(z + s <= D - 1)
        def _():
            feature(a, 1, s - 1, z + s).wait_recv()

            @pl.when(has_left)
            def _():
                feature(a, 1, s, z + s).start()

    def multiply_step(a, s):
        @pl.when(z - s >= 0)
        def _():
            multiply(a, z - s, False)

        @pl.when(z + s <= D - 1)
        def _():
            multiply(a, z + s, False)

    load(0).wait()
    start_own(0)
    load(1).wait()

    def start_pool(s):
        @pl.when((s == z) & has_right)
        def _():
            feature(1, 0, 0, z).start()

        @pl.when((s == D - 1 - z) & has_left)
        def _():
            feature(1, 1, 0, z).start()

    start_pool(0)
    load_w.wait()
    multiply(0, z, True)

    def target_step(s, carry):
        gather_step(0, s)
        start_pool(s)
        multiply_step(0, s)
        return carry

    lax.fori_loop(1, D, target_step, 0)
    probabilities(store_target)
    multiply(1, z, True)
    share_own().start()
    for j in range(1, D):
        share(j).start()

    def pool_step(s, carry):
        gather_step(1, s)
        multiply_step(1, s)

        @pl.when(s == max(1, D - 2))
        def _():
            share_own().wait()
            for j in range(1, D):
                share_in(j).wait_recv()
            for j in range(1, pairs):
                across(j, r, lax.rem(r + 2 * j, R)).start()
            beside(0, r).start()

        return carry

    lax.fori_loop(1, D, pool_step, 0)
    probabilities(store_pool)

    ones = jnp.ones((8, K), jnp.bfloat16)

    def fold_lanes(row):
        total = row
        for j in range(1, fold):
            total = total + pltpu.roll(row, j * part, 1)
        return total

    def entropy_rows(ref, first):
        def add(g, carry):
            mean = jnp.dot(ones, ref[first, g], preferred_element_type=jnp.float32) * (1.0 / K)
            return carry + xlogx(mean)

        return lax.fori_loop(0, groups, add, jnp.zeros((8, LANES), jnp.float32))

    def joint(chunk):
        def turn(g, carry):
            block = pool_full[chunk, g].T.astype(jnp.float32) * (1.0 / K)
            pool_turned[pl.ds(pl.multiple_of(g * LANES, LANES), LANES), :] = block.astype(
                jnp.bfloat16
            )
            return carry

        lax.fori_loop(0, groups, turn, 0)
        joint_sum[...] = jnp.zeros_like(joint_sum)
        double = math.gcd(groups, 8)
        tall = 256

        def column(i, carry):
            piece = lax.div(i, groups // double)
            g = lax.rem(i, groups // double) * double
            block = jnp.concatenate([target_full[piece, g + b] for b in range(double)], axis=1)
            total = None
            for top in range(0, groups * LANES, tall):
                value = xlogx(
                    jnp.dot(
                        pool_turned[top : top + tall, :], block, preferred_element_type=jnp.float32
                    )
                )
                for u in range(0, tall, LANES):
                    for v in range(0, double * LANES, LANES):
                        term = value[u : u + LANES, v : v + LANES]
                        total = term if total is None else total + term
            joint_sum[...] += total
            return carry

        lax.fori_loop(0, R * groups // double, column, 0)
        summed = jnp.sum(joint_sum[...].T, axis=0, keepdims=True)
        totals[0, chunk] = fold_lanes(jnp.broadcast_to(summed, (8, LANES)))
        totals[1, chunk] = fold_lanes(entropy_rows(pool_full, chunk))

    def finish_targets():
        for j in range(1, pairs):
            piece = lax.rem(r + R - 2 * j, R)
            across(j, piece, piece).wait_recv()
            beside(j, piece).start()
        for j in range(pairs):
            beside(j, lax.rem(partner + R - 2 * j, R)).wait_recv()

    def pool_round(t, carry):
        for s in range(D):
            chunk = t - s
            valid = (chunk >= 0) & (chunk < D)

            @pl.when(valid & (z - s >= 0))
            def _():
                if s:
                    pool_copy(0, s - 1, z - s, chunk).wait_recv()
                if s < D - 1:
                    @pl.when(has_right)
                    def _():
                        pool_copy(0, s, z - s, chunk).start()

            @pl.when(valid & (z + s <= D - 1))
            def _():
                if s:
                    pool_copy(1, s - 1, z + s, chunk).wait_recv()
                if s < D - 1:
                    @pl.when(has_left)
                    def _():
                        pool_copy(1, s, z + s, chunk).start()

        @pl.when(t == D - 1)
        def _():
            finish_targets()

        @pl.when(t >= D - 1)
        def _():
            joint(t - (D - 1))

        return carry

    lax.fori_loop(0, 2 * D - 1, pool_round, 0)

    def target_entropy(piece, carry):
        return carry + entropy_rows(target_full, piece)

    sums = lax.fori_loop(0, R, target_entropy, jnp.zeros((8, LANES), jnp.float32))
    targets_sum = jnp.sum(sums) * 0.125

    seg8 = lax.div(lax.broadcasted_iota(jnp.int32, (8, LANES), 1), part)

    def laid(which, h):
        row = totals[which, h * fold]
        for q in range(1, fold):
            row = jnp.where(seg8 == q, totals[which, h * fold + q], row)
        return row

    for h in range(halves):
        stage[h] = laid(0, h) - targets_sum
    keep = pltpu.make_async_copy(stage, final.at[z], l_sem.at[1])
    keep.start()
    keep.wait()

    def total_copy(j, owner, there):
        return pltpu.make_async_remote_copy(
            src_ref=final.at[owner],
            dst_ref=final.at[owner],
            send_sem=t_send.at[j - 1],
            recv_sem=t_recv.at[j - 1],
            device_id=(r, there),
            device_id_type=MESH,
        )

    for j in range(1, D):
        total_copy(j, z, lax.rem(z + j, D)).start()

    def ended(s, carry):
        for a in range(2):
            @pl.when((z - s >= 0) & has_right)
            def _():
                feature(a, 0, s, z - s).wait_send()

            @pl.when((z + s <= D - 1) & has_left)
            def _():
                feature(a, 1, s, z + s).wait_send()

        for chunk in range(D):
            @pl.when((z - s >= 0) & has_right)
            def _():
                pool_copy(0, s, z - s, chunk).wait_send()

            @pl.when((z + s <= D - 1) & has_left)
            def _():
                pool_copy(1, s, z + s, chunk).wait_send()

        return carry

    lax.fori_loop(0, D - 1, ended, 0)
    for j in range(1, D):
        share(j).wait_send()
    for j in range(1, pairs):
        across(j, r, lax.rem(r + 2 * j, R)).wait_send()
    for j in range(pairs):
        beside(j, lax.rem(r + R - 2 * j, R)).wait_send()
    for j in range(1, D):
        there = lax.rem(z + D - j, D)
        total_copy(j, there, there).wait_recv()
    for j in range(1, D):
        total_copy(j, z, lax.rem(z + j, D)).wait_send()
    scale = 1.0 / (R * part * D)
    for h in range(halves):
        total = final[0, h]
        for d in range(1, D):
            total = total + final[d, h]
        out_ref[h] = total * scale - laid(1, h)


def local(R, D, pool_inputs, target_inputs, class_weights, class_bias):
    rows, depth = pool_inputs.shape
    features, columns = class_weights.shape
    heads = columns // C
    K = heads * D
    part = rows // D
    fold = LANES // part
    groups = C // fold
    halves = rows // LANES
    bf16, f32 = jnp.bfloat16, jnp.float32
    DMA = pltpu.SemaphoreType.DMA
    anywhere = pl.BlockSpec(memory_space=pl.ANY)
    out = pl.pallas_call(
        functools.partial(kernel, R, D),
        out_shape=jax.ShapeDtypeStruct((halves, 8, LANES), f32),
        in_specs=[anywhere, anywhere, anywhere, pl.BlockSpec(memory_space=pltpu.VMEM)],
        out_specs=pl.BlockSpec(memory_space=pltpu.VMEM),
        scratch_shapes=[
            pltpu.VMEM((features, columns), bf16),
            pltpu.VMEM((2, D, rows, depth), bf16),
            pltpu.VMEM((rows, columns), f32),
            pltpu.VMEM((halves, columns, LANES), f32),
            pltpu.VMEM((D, groups, heads, LANES), bf16),
            pltpu.VMEM((D, groups, K, LANES), bf16),
            pltpu.VMEM((groups * LANES, K), bf16),
            pltpu.VMEM((R, groups, K, LANES), bf16),
            pltpu.VMEM((LANES, LANES), f32),
            pltpu.VMEM((2, D, 8, LANES), f32),
            pltpu.VMEM((halves, 8, LANES), f32),
            pltpu.VMEM((D, halves, 8, LANES), f32),
            DMA((3,)),
            DMA((2, 2, D - 1)),
            DMA((2, 2, D - 1)),
            DMA((D - 1,)),
            DMA((D - 1,)),
            DMA((R // 2 - 1,)),
            DMA((R // 2 - 1,)),
            DMA((R // 2,)),
            DMA((R // 2,)),
            DMA((2, D - 1, D)),
            DMA((2, D - 1, D)),
            DMA((2,)),
            DMA((D - 1,)),
            DMA((D - 1,)),
        ],
        compiler_params=pltpu.CompilerParams(collective_id=0, has_side_effects=True),
        name="gain",
    )(pool_inputs, target_inputs, class_weights, class_bias.reshape(1, columns))
    return out[:, 0, :].reshape(rows)


def solution(mesh):
    R, D = mesh.shape["rows"], mesh.shape["draws"]
    placed = (P("rows", "draws"), P("rows", "draws"), P(None, "draws"), P("draws"))
    return jax.shard_map(
        functools.partial(local, R, D),
        mesh=mesh,
        in_specs=placed,
        out_specs=P("rows"),
        check_vma=False,
    )
```

```python
import functools
import math

import jax
import jax.numpy as jnp
from jax import lax
from jax.experimental import pallas as pl
from jax.experimental.pallas import tpu as pltpu
from jax.sharding import PartitionSpec as P

C = 16
LANES = 128
MESH = pl.DeviceIdType.MESH
TINY = 1.1754944e-38


def xlogx(value):
    return value * jnp.log(jnp.maximum(value, TINY))


def kernel(
    R, D, pool_ref, target_ref, weights_ref, bias_ref, out_ref,
    w, gx, logits, turned, target_local, pool_full, pool_turned, target_full,
    joint_sum, totals, stage, final,
    in_sem, f_send, f_recv, a_send, a_recv, r_send, r_recv, c_send, c_recv,
    p_send, p_recv, l_sem, t_send, t_recv,
):
    r = lax.axis_index("rows")
    z = lax.axis_index("draws")
    rows, depth = gx.shape[2], gx.shape[3]
    columns = w.shape[1]
    heads = columns // C
    K = heads * D
    part = rows // D
    fold = LANES // part
    groups = C // fold
    halves = rows // LANES
    partner = r + 1 - 2 * lax.rem(r, 2)
    pairs = R // 2
    has_right = z < D - 1
    has_left = z > 0

    inputs = (target_ref, pool_ref)

    def load(a):
        return pltpu.make_async_copy(inputs[a], gx.at[a, z], in_sem.at[a])

    load_w = pltpu.make_async_copy(weights_ref, w, in_sem.at[2])
    load(0).start()
    load(1).start()
    load_w.start()

    barrier = pltpu.get_barrier_semaphore()
    for j in range(1, D):
        pl.semaphore_signal(barrier, inc=1, device_id=(r, lax.rem(z + j, D)), device_id_type=MESH)
    for j in range(1, pairs):
        pl.semaphore_signal(barrier, inc=1, device_id=(lax.rem(r + 2 * j, R), z), device_id_type=MESH)
    pl.semaphore_signal(barrier, inc=1, device_id=(partner, z), device_id_type=MESH)
    pl.semaphore_wait(barrier, D - 1 + pairs)

    def feature(a, way, hop, owner):
        return pltpu.make_async_remote_copy(
            src_ref=gx.at[a, owner],
            dst_ref=gx.at[a, owner],
            send_sem=f_send.at[a, way, hop],
            recv_sem=f_recv.at[a, way, hop],
            device_id=(r, z + 1 - 2 * way),
            device_id_type=MESH,
        )

    def share(j):
        there = lax.rem(z + j, D)
        return pltpu.make_async_remote_copy(
            src_ref=target_local.at[there],
            dst_ref=target_full.at[r, :, pl.ds(pl.multiple_of(z * heads, heads), heads), :],
            send_sem=a_send.at[j - 1],
            recv_sem=a_recv.at[j - 1],
            device_id=(r, there),
            device_id_type=MESH,
        )

    def share_in(j):
        there = lax.rem(z + D - j, D)
        at = pl.ds(pl.multiple_of(there * heads, heads), heads)
        return pltpu.make_async_remote_copy(
            src_ref=target_local.at[there],
            dst_ref=target_full.at[r, :, at, :],
            send_sem=a_send.at[j - 1],
            recv_sem=a_recv.at[j - 1],
            device_id=(r, there),
            device_id_type=MESH,
        )

    def share_own():
        return pltpu.make_async_copy(
            target_local.at[z],
            target_full.at[r, :, pl.ds(pl.multiple_of(z * heads, heads), heads), :],
            l_sem.at[0],
        )

    def across(j, piece, there):
        return pltpu.make_async_remote_copy(
            src_ref=target_full.at[piece],
            dst_ref=target_full.at[piece],
            send_sem=r_send.at[j - 1],
            recv_sem=r_recv.at[j - 1],
            device_id=(there, z),
            device_id_type=MESH,
        )

    def beside(j, piece):
        return pltpu.make_async_remote_copy(
            src_ref=target_full.at[piece],
            dst_ref=target_full.at[piece],
            send_sem=c_send.at[j],
            recv_sem=c_recv.at[j],
            device_id=(partner, z),
            device_id_type=MESH,
        )

    def pool_copy(way, hop, owner, chunk):
        at = pl.ds(pl.multiple_of(owner * heads, heads), heads)
        return pltpu.make_async_remote_copy(
            src_ref=pool_full.at[chunk, :, at, :],
            dst_ref=pool_full.at[chunk, :, at, :],
            send_sem=p_send.at[way, hop, chunk],
            recv_sem=p_recv.at[way, hop, chunk],
            device_id=(r, z + 1 - 2 * way),
            device_id_type=MESH,
        )

    wide = min(columns, 256)

    def multiply(a, owner, first):
        base = pl.multiple_of(owner * depth, depth)

        def tile(j, carry):
            at = pl.ds(pl.multiple_of(j * wide, wide), wide)
            product = jnp.dot(
                gx[a, owner], w[pl.ds(base, depth), at], preferred_element_type=jnp.float32
            )
            if first:
                logits[:, at] = product + bias_ref[:, at]
            else:
                logits[:, at] += product
            return carry

        lax.fori_loop(0, columns // wide, tile, 0)

    lane = lax.broadcasted_iota(jnp.int32, (16, LANES), 1)
    segment = lax.div(lane, part)

    def probabilities(store):
        def turn(j, carry):
            at = pl.ds(pl.multiple_of(j * LANES, LANES), LANES)
            for h in range(halves):
                turned[h, at, :] = logits[h * LANES : (h + 1) * LANES, at].T
            return carry

        lax.fori_loop(0, columns // LANES, turn, 0)

        def some(k, carry):
            for h in range(halves):
                values = [
                    turned[h, pl.ds(k * 16 * C + c, 16, stride=C), :] for c in range(C)
                ]
                top = functools.reduce(jnp.maximum, values)
                values = [jnp.exp(v - top) for v in values]
                scale = 1.0 / functools.reduce(jnp.add, values)
                values = [v * scale for v in values]
                for g in range(groups):
                    for q in range(fold):
                        mixed = values[g * fold]
                        if q:
                            mixed = pltpu.roll(mixed, (LANES - q * part) % LANES, 1)
                        for j in range(1, fold):
                            other = values[g * fold + j]
                            shift = ((j - q) * part) % LANES
                            if shift:
                                other = pltpu.roll(other, shift, 1)
                            mixed = jnp.where(segment == j, other, mixed)
                        store(h * fold + q, g, pl.multiple_of(k * 16, 16), mixed.astype(jnp.bfloat16))
            return carry

        lax.fori_loop(0, heads // 16, some, 0)

    def store_target(chunk, g, k, value):
        target_local[chunk, g, pl.ds(k, 16), :] = value

    def store_pool(chunk, g, k, value):
        pool_full[chunk, g, pl.ds(pl.multiple_of(z * heads + k, 16), 16), :] = value

    def start_own(a):
        @pl.when(has_right)
        def _():
            feature(a, 0, 0, z).start()

        @pl.when(has_left)
        def _():
            feature(a, 1, 0, z).start()

    def gather_step(a, s):
        @pl.when(z - s >= 0)
        def _():
            feature(a, 0, s - 1, z - s).wait_recv()

            @pl.when(has_right)
            def _():
                feature(a, 0, s, z - s).start()

        @pl.when(z + s <= D - 1)
        def _():
            feature(a, 1, s - 1, z + s).wait_recv()

            @pl.when(has_left)
            def _():
                feature(a, 1, s, z + s).start()

    def multiply_step(a, s):
        @pl.when(z - s >= 0)
        def _():
            multiply(a, z - s, False)

        @pl.when(z + s <= D - 1)
        def _():
            multiply(a, z + s, False)

    load(0).wait()
    start_own(0)
    load(1).wait()

    def start_pool(s):
        @pl.when((s == z) & has_right)
        def _():
            feature(1, 0, 0, z).start()

        @pl.when((s == D - 1 - z) & has_left)
        def _():
            feature(1, 1, 0, z).start()

    start_pool(0)
    load_w.wait()
    multiply(0, z, True)

    def target_step(s, carry):
        gather_step(0, s)
        start_pool(s)
        multiply_step(0, s)
        return carry

    lax.fori_loop(1, D, target_step, 0)
    probabilities(store_target)
    multiply(1, z, True)
    share_own().start()
    for j in range(1, D):
        share(j).start()

    def pool_step(s, carry):
        gather_step(1, s)
        multiply_step(1, s)

        @pl.when(s == max(1, D - 2))
        def _():
            share_own().wait()
            for j in range(1, D):
                share_in(j).wait_recv()
            for j in range(1, pairs):
                across(j, r, lax.rem(r + 2 * j, R)).start()
            beside(0, r).start()

        return carry

    lax.fori_loop(1, D, pool_step, 0)
    probabilities(store_pool)

    ones = jnp.ones((8, K), jnp.bfloat16)

    def fold_lanes(row):
        total = row
        for j in range(1, fold):
            total = total + pltpu.roll(row, j * part, 1)
        return total

    def entropy_rows(ref, first):
        def add(g, carry):
            mean = jnp.dot(ones, ref[first, g], preferred_element_type=jnp.float32) * (1.0 / K)
            return carry + xlogx(mean)

        total = jnp.zeros((8, LANES), jnp.float32)
        for g in range(groups):
            total = add(g, total)
        return total

    def joint(chunk):
        def turn(g, carry):
            block = pool_full[chunk, g].T.astype(jnp.float32) * (1.0 / K)
            pool_turned[pl.ds(pl.multiple_of(g * LANES, LANES), LANES), :] = block.astype(
                jnp.bfloat16
            )
            return carry

        lax.fori_loop(0, groups, turn, 0)
        joint_sum[...] = jnp.zeros_like(joint_sum)
        double = math.gcd(groups, 8)
        tall = 256

        def column(i, carry):
            piece = lax.div(i, groups // double)
            g = lax.rem(i, groups // double) * double
            block = jnp.concatenate([target_full[piece, g + b] for b in range(double)], axis=1)
            total = None
            for top in range(0, groups * LANES, tall):
                value = xlogx(
                    jnp.dot(
                        pool_turned[top : top + tall, :], block, preferred_element_type=jnp.float32
                    )
                )
                for u in range(0, tall, LANES):
                    for v in range(0, double * LANES, LANES):
                        term = value[u : u + LANES, v : v + LANES]
                        total = term if total is None else total + term
            joint_sum[...] += total
            return carry

        lax.fori_loop(0, R * groups // double, column, 0)
        summed = jnp.sum(joint_sum[...].T, axis=0, keepdims=True)
        totals[0, chunk] = fold_lanes(jnp.broadcast_to(summed, (8, LANES)))
        totals[1, chunk] = fold_lanes(entropy_rows(pool_full, chunk))

    def finish_targets():
        for j in range(1, pairs):
            piece = lax.rem(r + R - 2 * j, R)
            across(j, piece, piece).wait_recv()
            beside(j, piece).start()
        for j in range(pairs):
            beside(j, lax.rem(partner + R - 2 * j, R)).wait_recv()

    def pool_round(t, carry):
        for s in range(D):
            chunk = t - s
            valid = (chunk >= 0) & (chunk < D)

            @pl.when(valid & (z - s >= 0))
            def _():
                if s:
                    pool_copy(0, s - 1, z - s, chunk).wait_recv()
                if s < D - 1:
                    @pl.when(has_right)
                    def _():
                        pool_copy(0, s, z - s, chunk).start()

            @pl.when(valid & (z + s <= D - 1))
            def _():
                if s:
                    pool_copy(1, s - 1, z + s, chunk).wait_recv()
                if s < D - 1:
                    @pl.when(has_left)
                    def _():
                        pool_copy(1, s, z + s, chunk).start()

        @pl.when(t == min(1, D - 1))
        def _():
            for j in range(1, pairs):
                piece = lax.rem(r + R - 2 * j, R)
                across(j, piece, piece).wait_recv()
                beside(j, piece).start()

        @pl.when(t == D - 1)
        def _():
            for j in range(pairs):
                beside(j, lax.rem(partner + R - 2 * j, R)).wait_recv()

        @pl.when(t >= D - 1)
        def _():
            joint(t - (D - 1))

        return carry

    lax.fori_loop(0, 2 * D - 1, pool_round, 0)

    def target_entropy(piece, carry):
        return carry + entropy_rows(target_full, piece)

    sums = lax.fori_loop(0, R, target_entropy, jnp.zeros((8, LANES), jnp.float32))
    targets_sum = jnp.sum(sums) * 0.125

    seg8 = lax.div(lax.broadcasted_iota(jnp.int32, (8, LANES), 1), part)

    def laid(which, h):
        row = totals[which, h * fold]
        for q in range(1, fold):
            row = jnp.where(seg8 == q, totals[which, h * fold + q], row)
        return row

    for h in range(halves):
        stage[h] = laid(0, h) - targets_sum
    keep = pltpu.make_async_copy(stage, final.at[z], l_sem.at[1])
    keep.start()
    keep.wait()

    def total_copy(j, owner, there):
        return pltpu.make_async_remote_copy(
            src_ref=final.at[owner],
            dst_ref=final.at[owner],
            send_sem=t_send.at[j - 1],
            recv_sem=t_recv.at[j - 1],
            device_id=(r, there),
            device_id_type=MESH,
        )

    for j in range(1, D):
        total_copy(j, z, lax.rem(z + j, D)).start()

    def ended(s, carry):
        for a in range(2):
            @pl.when((z - s >= 0) & has_right)
            def _():
                feature(a, 0, s, z - s).wait_send()

            @pl.when((z + s <= D - 1) & has_left)
            def _():
                feature(a, 1, s, z + s).wait_send()

        for chunk in range(D):
            @pl.when((z - s >= 0) & has_right)
            def _():
                pool_copy(0, s, z - s, chunk).wait_send()

            @pl.when((z + s <= D - 1) & has_left)
            def _():
                pool_copy(1, s, z + s, chunk).wait_send()

        return carry

    lax.fori_loop(0, D - 1, ended, 0)
    for j in range(1, D):
        share(j).wait_send()
    for j in range(1, pairs):
        across(j, r, lax.rem(r + 2 * j, R)).wait_send()
    for j in range(pairs):
        beside(j, lax.rem(r + R - 2 * j, R)).wait_send()
    for j in range(1, D):
        there = lax.rem(z + D - j, D)
        total_copy(j, there, there).wait_recv()
    for j in range(1, D):
        total_copy(j, z, lax.rem(z + j, D)).wait_send()
    scale = 1.0 / (R * part * D)
    for h in range(halves):
        total = final[0, h]
        for d in range(1, D):
            total = total + final[d, h]
        out_ref[h] = total * scale - laid(1, h)


def local(R, D, pool_inputs, target_inputs, class_weights, class_bias):
    rows, depth = pool_inputs.shape
    features, columns = class_weights.shape
    heads = columns // C
    K = heads * D
    part = rows // D
    fold = LANES // part
    groups = C // fold
    halves = rows // LANES
    bf16, f32 = jnp.bfloat16, jnp.float32
    DMA = pltpu.SemaphoreType.DMA
    anywhere = pl.BlockSpec(memory_space=pl.ANY)
    out = pl.pallas_call(
        functools.partial(kernel, R, D),
        out_shape=jax.ShapeDtypeStruct((halves, 8, LANES), f32),
        in_specs=[anywhere, anywhere, anywhere, pl.BlockSpec(memory_space=pltpu.VMEM)],
        out_specs=pl.BlockSpec(memory_space=pltpu.VMEM),
        scratch_shapes=[
            pltpu.VMEM((features, columns), bf16),
            pltpu.VMEM((2, D, rows, depth), bf16),
            pltpu.VMEM((rows, columns), f32),
            pltpu.VMEM((halves, columns, LANES), f32),
            pltpu.VMEM((D, groups, heads, LANES), bf16),
            pltpu.VMEM((D, groups, K, LANES), bf16),
            pltpu.VMEM((groups * LANES, K), bf16),
            pltpu.VMEM((R, groups, K, LANES), bf16),
            pltpu.VMEM((LANES, LANES), f32),
            pltpu.VMEM((2, D, 8, LANES), f32),
            pltpu.VMEM((halves, 8, LANES), f32),
            pltpu.VMEM((D, halves, 8, LANES), f32),
            DMA((3,)),
            DMA((2, 2, D - 1)),
            DMA((2, 2, D - 1)),
            DMA((D - 1,)),
            DMA((D - 1,)),
            DMA((R // 2 - 1,)),
            DMA((R // 2 - 1,)),
            DMA((R // 2,)),
            DMA((R // 2,)),
            DMA((2, D - 1, D)),
            DMA((2, D - 1, D)),
            DMA((2,)),
            DMA((D - 1,)),
            DMA((D - 1,)),
        ],
        compiler_params=pltpu.CompilerParams(collective_id=0, has_side_effects=True),
        name="gain",
    )(pool_inputs, target_inputs, class_weights, class_bias.reshape(1, columns))
    return out[:, 0, :].reshape(rows)


def solution(mesh):
    R, D = mesh.shape["rows"], mesh.shape["draws"]
    placed = (P("rows", "draws"), P("rows", "draws"), P(None, "draws"), P("draws"))
    return jax.shard_map(
        functools.partial(local, R, D),
        mesh=mesh,
        in_specs=placed,
        out_specs=P("rows"),
        check_vma=False,
    )
```
